32 devices in a mesh: ka: 2 (over x), pts: 16 (over z, y, core).
Axes of the slice: x: 2, y: 2, z: 4, core: 2. Of those that a mesh axis runs over, the one named last changes fastest.
Arguments:
- orbitals: bfloat16 [216, 2, 4096, 384], P('ka', None, 'pts'), may hold values from -1.5 to 1.5
- counts: int32 [216], P('ka'), may hold values from 60 to 300
- occupation: float32 [216, 384], P('ka'), may hold values from 0.2 to 1
- coulomb: bfloat16 [216, 2, 16, 4096], P('ka', None, None, 'pts'), may hold values from -24 to 24
Outputs:
- exchange_block: bfloat16 [216, 2, 16, 4096], P('ka', None, None, 'pts')
The draws below stay inside these ranges and needn't reach their ends.
Inputs may be any that keep to these rules, and one draw needn't show every extreme that they name: `counts`: between 60 and 300 occupied bands per k-point.
All inputs are finite; a program needn't handle non-finite values.
Results may differ from the reference program's by a relative error of at most 0.0057.
Values may be sent and summed in bfloat16 or wider, within the bound.
No kernel may reach another device: no remote copies, remote signals or barrier semaphores. Data moves between devices by JAX's collectives and lax.ppermute only.
A program may use at most 128 MiB of HBM per device.

```python
import jax
import jax.numpy as jnp
from jax import lax

NMU = 4096
NB = 384
KSIDE = 6
ROW_DEV = 1
NK = 216
ROWS = 16
N_PTS = 16


def with_ends(drawn, own_key, smallest, top_value):
    shape = drawn.shape
    index_at = [jax.random.randint(jax.random.fold_in(own_key, axis), (), 0, shape[axis]) for axis in range(len(shape))]
    drawn = drawn.at[tuple(index_at)].set(smallest)
    longest = shape.index(max(shape))
    index_at[longest] = (index_at[longest] + 1) % shape[longest]
    return drawn.at[tuple(index_at)].set(top_value)


def block_scale(own_key, extent, shards, smallest, high):
    loudness, own = 1.0, jax.random.fold_in(own_key, 6)
    for position, blocks in shards:
        heights = jnp.exp(jax.random.uniform(jax.random.fold_in(own, position), (blocks,), jnp.float32, smallest / len(shards), high / len(shards)))
        loudness = loudness * jnp.repeat(heights, extent[position] // blocks).reshape([-1 if axis == position else 1 for axis in range(len(extent))])
    return loudness


def normal_values(key, extent, spread, most, cuts=(), kind=jnp.bfloat16):
    values = spread * jax.random.normal(key, extent, jnp.float32)
    if cuts:
        values = values * block_scale(key, extent, cuts, -0.22, 0.18)
    return jnp.clip(values, -most, most).astype(kind)


def setup_inputs(seed: int = 0) -> dict:
    streams_of = jax.random.split(jax.random.key(seed), 5)
    orbitals = normal_values(streams_of[0], (NK, 2, NMU, NB), 0.25, 1.5, ((0, 2), (2, 16)))
    counts = with_ends(jax.random.randint(streams_of[1], (NK,), 5 * NB // 32, 25 * NB // 32 + 1), jax.random.fold_in(streams_of[1], 1), 5 * NB // 32, (25 * NB // 32 + 1) - 1).astype(jnp.int32)
    occupation = jnp.clip(0.2 + 0.8 * jax.random.uniform(streams_of[2], (NK, NB), jnp.float32) ** block_scale(streams_of[2], (NK, NB), ((0, 2),), -0.2, 0.2), 0.2, 1.0)
    coulomb = normal_values(streams_of[3], (NK, 2, ROWS, NMU), 4.0, 24.0, ((0, 2), (3, 16)))
    return {"orbitals": orbitals, "counts": counts, "occupation": occupation, "coulomb": coulomb}


def slab_points():
    pts_dev = NMU // N_PTS
    rows = jnp.arange(ROWS, dtype=jnp.int32)
    return ((rows // ROW_DEV) * pts_dev + rows % ROW_DEV).astype(jnp.int32)


def reference(orbitals, counts, occupation, coulomb):
    band = jnp.arange(NB, dtype=jnp.int32)
    weights = jnp.where(band[None, :] < counts[:, None], occupation, jnp.float32(0.0)).astype(jnp.float32)
    slab = jnp.take(orbitals, slab_points(), axis=2).astype(jnp.float32)
    weighted = (slab * weights[:, None, None, :]).astype(jnp.bfloat16)
    weighted = lax.optimization_barrier(weighted).astype(jnp.float32)
    left_re = weighted[:, 0]
    left_im = weighted[:, 1]

    def one_block(start):
        cols = lax.dynamic_slice_in_dim(orbitals, start, 512, 2).astype(jnp.float32)
        right_re = cols[:, 0]
        right_im = cols[:, 1]
        real = jnp.einsum('krb,knb->krn', left_re, right_re) + jnp.einsum('krb,knb->krn', left_im, right_im)
        imag = jnp.einsum('krb,knb->krn', left_im, right_re) - jnp.einsum('krb,knb->krn', left_re, right_im)
        real = lax.optimization_barrier(real.astype(jnp.bfloat16)).astype(jnp.float32)
        imag = lax.optimization_barrier(imag.astype(jnp.bfloat16)).astype(jnp.float32)
        density = (real + 1j * imag).reshape(KSIDE, KSIDE, KSIDE, ROWS, 512)
        kernel = lax.dynamic_slice_in_dim(coulomb, start, 512, 3).astype(jnp.float32)
        kernel = (kernel[:, 0] + 1j * kernel[:, 1]).reshape(KSIDE, KSIDE, KSIDE, ROWS, 512)
        product = jnp.fft.fftn(kernel, axes=(0, 1, 2)) * jnp.fft.fftn(density, axes=(0, 1, 2))
        result = -jnp.fft.ifftn(product, axes=(0, 1, 2)) / NK
        result = result.reshape(NK, ROWS, 512)
        return jnp.stack([jnp.real(result), jnp.imag(result)], 1).astype(jnp.bfloat16)

    starts = (jnp.arange(NMU // 512, dtype=jnp.int32) * 512).astype(jnp.int32)
    blocks = lax.map(one_block, starts)
    blocks = jnp.moveaxis(blocks, 0, 3)
    return blocks.reshape(NK, 2, ROWS, NMU)
```

```python
import jax
import jax.numpy as jnp
from jax import lax
from jax.experimental import pallas as pl
from jax.experimental.pallas import tpu as pltpu
from jax.sharding import PartitionSpec as P

KSIDE = 6
ROW_DEV = 1
HALF = KSIDE // 2
LANES = 128
SUB = 8
ROOT = 0.8660254037844386


def pack_rows(table, parts):
    count, width = parts[0].shape
    rows = len(parts)
    tiles = width // LANES

    def kernel(table_ref, *refs):
        sources, out, flat = refs[:rows], refs[rows], refs[rows + 1]
        for start in range(0, count, SUB):
            size = min(SUB, count - start)
            for part in range(rows):
                block = sources[part][start : start + size, :].astype(jnp.float32)
                at = table_ref[part] + start * rows
                for tile in range(tiles):
                    flat[tile, pl.ds(at, size, stride=rows), :] = block[:, tile * LANES : (tile + 1) * LANES]

        def emit(k, _):
            for tile in range(tiles):
                out[k, :, tile * LANES : (tile + 1) * LANES] = flat[tile, pl.ds(pl.multiple_of(k * rows, rows), rows), :].astype(jnp.bfloat16)
            return 0

        lax.fori_loop(0, count, emit, 0, unroll=4)

    return pl.pallas_call(
        kernel,
        out_shape=jax.ShapeDtypeStruct((count, rows, width), jnp.bfloat16),
        grid_spec=pltpu.PrefetchScalarGridSpec(
            num_scalar_prefetch=1,
            grid=(1,),
            in_specs=[pl.BlockSpec((count, width), lambda i, t: (0, 0))] * rows,
            out_specs=pl.BlockSpec((count, rows, width), lambda i, t: (0, 0, 0)),
            scratch_shapes=[pltpu.VMEM((tiles, count * rows, LANES), jnp.float32)],
        ),
        name="pack_rows",
    )(table, *parts)


def density_half(left, orbitals, column, columns, step):
    count, rows, width = left.shape
    slots = width // 2
    keep = rows // 2

    def kernel(left_ref, orb_ref, keep_ref, send_ref):
        for k in range(step):
            re = left_ref[k, :, :slots]
            im = left_ref[k, :, slots:]
            dims = (((1,), (1,)), ((), ()))
            out = lax.dot_general(jnp.concatenate([re, im], 0), orb_ref[k, 0], dims, preferred_element_type=jnp.float32)
            out = out + lax.dot_general(jnp.concatenate([im, -re], 0), orb_ref[k, 1], dims, preferred_element_type=jnp.float32)
            out = out.astype(jnp.bfloat16)
            keep_ref[k, 0] = out[:keep]
            send_ref[k, 0] = out[keep:rows]
            keep_ref[k, 1] = out[rows : rows + keep]
            send_ref[k, 1] = out[rows + keep :]

    half = jax.ShapeDtypeStruct((count, 2, keep, columns), jnp.bfloat16)
    half_spec = pl.BlockSpec((step, 2, keep, columns), lambda i: (i, 0, 0, 0))
    return pl.pallas_call(
        kernel,
        out_shape=(half, half),
        grid=(count // step,),
        in_specs=[
            pl.BlockSpec((step, rows, width), lambda i: (i, 0, 0)),
            pl.BlockSpec((step, 2, columns, slots), lambda i: (i, 0, column, 0)),
        ],
        out_specs=(half_spec, half_spec),
        name="density_half",
    )(left, orbitals)


def add(a, b):
    return a[0] + b[0], a[1] + b[1]


def sub(a, b):
    return a[0] - b[0], a[1] - b[1]


def three(a, b, c, inverse):
    total = add(b, c)
    first = add(a, total)
    middle = a[0] - 0.5 * total[0], a[1] - 0.5 * total[1]
    turn = ROOT * (b[0] - c[0]), ROOT * (b[1] - c[1])
    low = middle[0] + turn[1], middle[1] - turn[0]
    high = middle[0] - turn[1], middle[1] + turn[0]
    return (first, high, low) if inverse else (first, low, high)


def six(x):
    u = three(add(x[0], x[3]), add(x[4], x[1]), add(x[2], x[5]), False)
    v = three(sub(x[0], x[3]), sub(x[4], x[1]), sub(x[2], x[5]), False)
    return list(u) + list(v)


def six_back(x):
    u = three(*x[:3], True)
    v = three(*x[3:], True)
    return [add(u[0], v[0]), sub(u[1], v[1]), add(u[2], v[2]), sub(u[0], v[0]), add(u[1], v[1]), sub(u[2], v[2])]


def first_pass(own, other, work, lanes):
    def load(ref, k):
        return ref[k, 0, :, lanes].astype(jnp.float32), ref[k, 1, :, lanes].astype(jnp.float32)

    def body(ky, _):
        for kx in range(HALF):
            base = (kx * KSIDE + ky) * KSIDE
            mine = [load(own, base + kz) for kz in range(KSIDE)]
            theirs = [load(other, base + kz) for kz in range(KSIDE)]
            plus = six([add(a, b) for a, b in zip(mine, theirs)])
            minus = six([sub(b, a) if kx % 2 else sub(a, b) for a, b in zip(mine, theirs)])
            for sign, values in enumerate((plus, minus)):
                for kz in range(KSIDE):
                    for part in range(2):
                        work[sign, kz, kx, ky, part] = values[kz][part]
        return 0

    lax.fori_loop(0, KSIDE, body, 0)


def plane_forward(work, sign, kz):
    grid = []
    for kx in range(HALF):
        grid.append(six([(work[sign, kz, kx, ky, 0], work[sign, kz, kx, ky, 1]) for ky in range(KSIDE)]))
    for ky in range(KSIDE):
        column = three(grid[0][ky], grid[1][ky], grid[2][ky], False)
        for kx in range(HALF):
            grid[kx][ky] = column[kx]
    return grid


def coulomb_transform(flip, own, other):
    count, _, rows, columns = own.shape
    tiles = columns // LANES
    scale = -0.5 / (HALF * HALF * HALF * 4 * KSIDE * KSIDE * KSIDE)

    def kernel(flip_ref, own_ref, other_ref, out_ref, work):
        first_pass(own_ref, other_ref, work, slice(None))

        def body(kz, _):
            for sign in range(2):
                factor = flip_ref[0] * scale if sign else jnp.float32(scale)
                grid = plane_forward(work, sign, kz)
                for kx in range(HALF):
                    for ky in range(KSIDE):
                        for part in range(2):
                            out_ref[sign, kz, kx, ky, part] = grid[kx][ky][part] * factor
            return 0

        lax.fori_loop(0, KSIDE, body, 0)

    shape = (2, KSIDE, HALF, KSIDE, 2, rows, columns)
    half_spec = pl.BlockSpec((count, 2, rows, LANES), lambda i: (0, 0, 0, i))
    return pl.pallas_call(
        kernel,
        out_shape=jax.ShapeDtypeStruct(shape, jnp.float32),
        grid=(tiles,),
        in_specs=[pl.BlockSpec(memory_space=pltpu.SMEM), half_spec, half_spec],
        out_specs=pl.BlockSpec(shape[:-1] + (LANES,), lambda i: (0,) * 6 + (i,)),
        scratch_shapes=[pltpu.VMEM(shape[:-1] + (LANES,), jnp.float32)],
        name="coulomb_transform",
    )(flip, own, other)


def convolve(own, other, kernel_hat, column):
    count, _, rows, columns = own.shape

    def kernel(own_ref, other_ref, hat, keep_ref, send_ref, work):
        first_pass(own_ref, other_ref, work, slice(None))

        def middle(kz, _):
            for sign in range(2):
                grid = plane_forward(work, sign, kz)
                for ky in range(KSIDE):
                    column_values = []
                    for kx in range(HALF):
                        a, b = grid[kx][ky]
                        c, d = hat[sign, kz, kx, ky, 0], hat[sign, kz, kx, ky, 1]
                        column_values.append((a * c - b * d, a * d + b * c))
                    column_values = three(*column_values, True)
                    for kx in range(HALF):
                        grid[kx][ky] = column_values[kx]
                for kx in range(HALF):
                    values = six_back(grid[kx])
                    for ky in range(KSIDE):
                        for part in range(2):
                            work[sign, kz, kx, ky, part] = values[ky][part]
            return 0

        lax.fori_loop(0, KSIDE, middle, 0)

        def last(ky, _):
            for kx in range(HALF):
                both = []
                for sign in range(2):
                    both.append(six_back([(work[sign, kz, kx, ky, 0], work[sign, kz, kx, ky, 1]) for kz in range(KSIDE)]))
                base = (kx * KSIDE + ky) * KSIDE
                for kz in range(KSIDE):
                    for part in range(2):
                        plus, minus = both[0][kz][part], both[1][kz][part]
                        if kx % 2:
                            minus = -minus
                        keep_ref[base + kz, part] = (plus + minus).astype(jnp.bfloat16)
                        send_ref[base + kz, part] = (plus - minus).astype(jnp.bfloat16)
            return 0

        lax.fori_loop(0, KSIDE, last, 0)

    shape = (2, KSIDE, HALF, KSIDE, 2, rows, columns)
    half = jax.ShapeDtypeStruct(own.shape, jnp.bfloat16)
    half_spec = pl.BlockSpec(own.shape, lambda i: (0, 0, 0, 0))
    return pl.pallas_call(
        kernel,
        out_shape=(half, half),
        grid=(1,),
        in_specs=[half_spec, half_spec, pl.BlockSpec(shape, lambda i: (0,) * 6 + (column,))],
        out_specs=(half_spec, half_spec),
        scratch_shapes=[pltpu.VMEM(shape, jnp.float32)],
        name="convolve",
    )(own, other, kernel_hat)


def band_gram(left, right):

    def product(first, second):
        return jnp.einsum("krb,knb->krn", first, second, preferred_element_type=jnp.float32)

    real = product(left[:, 0], right[:, 0]) + product(left[:, 1], right[:, 1])
    imag = product(left[:, 1], right[:, 0]) - product(left[:, 0], right[:, 1])
    return jnp.stack([real, imag], 1)


def side_table(sign):
    index = jnp.arange(KSIDE, dtype=jnp.int32)
    phase = index[:, None] * index[None, :] % KSIDE
    angle = phase.astype(jnp.float32) * (2.0 * jnp.pi / KSIDE)
    cosine = jnp.cos(angle)
    sine = jnp.sin(angle) * sign
    top = jnp.stack([cosine, sine], 2)
    bottom = jnp.stack([-sine, cosine], 2)
    return jnp.stack([top, bottom], 1)


def mesh_transform(values, sign):
    table = side_table(sign)
    forms = ["acbd,bxydm->axycm", "acbd,xbydm->xaycm", "acbd,xybdm->xyacm"]
    for form in forms:
        values = jnp.einsum(
            form, table, values, precision=lax.Precision.HIGHEST, preferred_element_type=jnp.float32
        )
    return values


def convolve_any(density, kernel):
    shape = density.shape
    count = shape[0]
    dens = mesh_transform(density.astype(jnp.float32).reshape(KSIDE, KSIDE, KSIDE, 2, -1), 1.0)
    kern = mesh_transform(kernel.astype(jnp.float32).reshape(KSIDE, KSIDE, KSIDE, 2, -1), 1.0)
    prod_re = kern[:, :, :, 0] * dens[:, :, :, 0] - kern[:, :, :, 1] * dens[:, :, :, 1]
    prod_im = kern[:, :, :, 0] * dens[:, :, :, 1] + kern[:, :, :, 1] * dens[:, :, :, 0]
    back = mesh_transform(jnp.stack([prod_re, prod_im], 3), -1.0)
    scale = -1.0 / (count * count)
    return (back * scale).reshape(shape).astype(jnp.bfloat16)


def slab_rows(orbitals, counts, occupation):
    slots = orbitals.shape[3]
    band = jnp.arange(slots, dtype=jnp.int32)
    weights = jnp.where(band[None, :] < counts[:, None], occupation, jnp.float32(0.0))
    return (orbitals[:, :, :ROW_DEV, :].astype(jnp.float32) * weights[:, None, None, :]).astype(
        jnp.bfloat16
    )


def local_any(orbitals, counts, occupation, coulomb):
    weighted = slab_rows(orbitals, counts, occupation)
    gathered = lax.all_gather(weighted, "pts", axis=2, tiled=True)
    density = band_gram(gathered, orbitals).astype(jnp.bfloat16)
    result = convolve_any(
        lax.all_to_all(density, "ka", split_axis=3, concat_axis=0, tiled=True),
        lax.all_to_all(coulomb, "ka", split_axis=3, concat_axis=0, tiled=True),
    )
    return lax.all_to_all(result, "ka", split_axis=0, concat_axis=3, tiled=True)


def gather_rows(block, ring):
    side = ring * 4

    def move(value, dest):
        pairs = []
        for z in range(ring):
            for y in range(2):
                for core in range(2):
                    to_z, to_y, to_core = dest(z, y, core)
                    pairs.append(((z * 2 + y) * 2 + core, (to_z % ring * 2 + to_y) * 2 + to_core))
        return lax.ppermute(value, "pts", pairs)

    def twin(z, y, core):
        return z, y, 1 - core

    def along(z, y, core):
        return z + 1 - 2 * core, y, core

    def across(z, y, core):
        return z, 1 - y, core

    def corner(z, y, core):
        return z + 1 - 2 * core, 1 - y, core

    here = lax.axis_index("pts")
    core = here % 2
    y = here // 2 % 2
    z = here // 4

    def index(dz, flip_y, of_core):
        return ((z + dz) % ring * 2 + (1 - y if flip_y else y)) * 2 + of_core

    back = 2 * core - 1
    near = move(block, twin)
    side_own = move(block, along)
    corner_own = move(block, corner)
    across_own = move(block, across)
    side_twin = move(near, along)
    corner_twin = move(near, corner)
    far = move(side_own, along)
    far_corner = move(corner_own, along)
    received = [
        (side_own, back, 0, core),
        (side_twin, back, 0, 1 - core),
        (corner_own, back, 1, core),
        (corner_twin, back, 1, 1 - core),
        (across_own, 0, 1, core),
        (far, 2 * back, 0, core),
        (far_corner, 2 * back, 1, core),
    ]
    parts = [block, near]
    where = [index(0, 0, core), index(0, 0, 1 - core)]
    for value, dz, flip_y, of_core in received:
        parts.append(value)
        where.append(index(dz, flip_y, of_core))
        parts.append(move(value, twin))
        where.append(index(-dz, flip_y, 1 - of_core))
    return parts, jnp.stack(where)


def local_pair(orbitals, counts, occupation, coulomb):
    swap = [(0, 1), (1, 0)]
    count, _, columns, slots = orbitals.shape
    rows = coulomb.shape[2]
    keep = rows // 2
    half = lax.axis_index("ka")

    def part_of(value, which):
        return lax.dynamic_slice_in_dim(value, which * keep, keep, 2)

    other_coulomb = lax.ppermute(part_of(coulomb, 1 - half), "ka", swap)
    block = slab_rows(orbitals, counts, occupation).reshape(count, 2 * slots)
    parts, where = gather_rows(block, lax.axis_size("pts") // 4)
    where = ((where + keep * half) % rows).astype(jnp.int32)
    left = pack_rows(where, parts)
    flip = jnp.where(half == 0, 1.0, -1.0).astype(jnp.float32).reshape(1)
    hat = coulomb_transform(flip, part_of(coulomb, half), other_coulomb)
    steps = [density_half(left, orbitals, j, LANES, 12) for j in range(columns // LANES)]
    others = [lax.ppermute(sent, "ka", swap) for _, sent in steps]
    done = [convolve(steps[j][0], others[j], hat, j) for j in range(columns // LANES)]
    kept = jnp.concatenate([keep_part for keep_part, _ in done], 3)
    back = jnp.concatenate([lax.ppermute(sent, "ka", swap) for _, sent in done], 3)
    return jnp.where(half == 0, jnp.concatenate([kept, back], 2), jnp.concatenate([back, kept], 2))


def solution(mesh):
    pair = mesh.shape["ka"] == 2 and mesh.shape["pts"] == 16

    def local(orbitals, counts, occupation, coulomb):
        columns = orbitals.shape[2]
        if pair and columns % LANES == 0 and orbitals.shape[0] % (HALF * KSIDE * KSIDE) == 0:
            return local_pair(orbitals, counts, occupation, coulomb)
        return local_any(orbitals, counts, occupation, coulomb)

    return jax.shard_map(
        local,
        mesh=mesh,
        in_specs=(P("ka", None, "pts", None), P("ka"), P("ka", None), P("ka", None, None, "pts")),
        out_specs=P("ka", None, None, "pts"),
        check_vma=False,
    )
```

```python
import jax
import jax.numpy as jnp
from jax import lax
from jax.experimental import pallas as pl
from jax.experimental.pallas import tpu as pltpu
from jax.sharding import PartitionSpec as P


KSIDE = 6
ROW_DEV = 1
HALF = KSIDE // 2
LANES = 128
ROOT = 0.8660254037844386


LANE_HALF = LANES // 2
GROUP = 6
AHEAD = 2
BLOCK = 16


def band_order(counts, parts):
    tiles = -(-counts.reshape(parts, -1) // LANES)
    size = tiles.shape[1]
    index = jnp.arange(size, dtype=jnp.int32)
    key = tiles * size - index
    rank = jnp.sum((key[:, None, :] > key[:, :, None]).astype(jnp.int32), 2)
    hit = (rank[:, :, None] == index).astype(jnp.int32)
    return jnp.sum(hit * index[:, None], 1), jnp.sum(hit * tiles[:, :, None], 1)


def density_part(spread, order, tiles, parts, orbitals, start, count):
    rows = len(parts)
    width = parts[0].shape[1]
    columns, slots = orbitals.shape[2:]
    keep = rows // 2
    first = start // BLOCK * BLOCK
    span = -(-(start + count - first) // BLOCK) * BLOCK
    group = GROUP
    ahead = AHEAD
    groups = count // group
    ring = ahead + 1
    whole = (slots // LANES - 1) * LANES
    depth = slots // LANES
    splits = columns // LANES

    def kernel(order_ref, tiles_ref, spread_ref, *refs):
        sources, orb, refs = refs[:rows], refs[rows], refs[rows + 1 :]
        keep_ref, send_refs, (raw, left, buf, raw_sem, sem) = refs[0], refs[1 : 1 + splits], refs[1 + splits :]
        row_copies = [
            pltpu.make_async_copy(sources[i].at[pl.ds(first, span)], raw.at[i], raw_sem.at[i]) for i in range(rows)
        ]

        def per_class(g, act):
            for n in range(1, depth + 1):
                pl.when(tiles_ref[g * group] == n)(lambda n=n: act(n))

        def panels(g, n, act):
            lanes = pl.ds(0, n * LANES)
            for u in range(group):
                slot = g % ring * group + u
                source = orb.at[start + order_ref[g * group + u], :, :, lanes]
                act(pltpu.make_async_copy(source, buf.at[slot, :, :, lanes], sem.at[slot]))

        for copy in row_copies:
            copy.start()
        for g in range(min(ahead, groups)):
            per_class(g, lambda n, g=g: panels(g, n, lambda copy: copy.start()))
        for copy in row_copies:
            copy.wait()
        lane = lax.broadcasted_iota(jnp.int32, (BLOCK * rows, LANES), 1)
        for at in range(0, span, BLOCK):
            stacked = jnp.concatenate([raw[i, at : at + BLOCK, :] for i in range(rows)], 0)
            mixed = jnp.dot(spread_ref[...], stacked, preferred_element_type=jnp.float32)
            last = mixed[:, 2 * whole :]
            re_last = jnp.where(lane < LANE_HALF, last, 0.0)
            im_last = jnp.where(lane < LANE_HALF, pltpu.roll(last, LANE_HALF, 1), 0.0)
            pieces = [mixed[:, :whole], re_last, mixed[:, whole : 2 * whole], im_last]
            left[at * rows : (at + BLOCK) * rows, :] = jnp.concatenate(pieces, 1).astype(jnp.bfloat16)
        dims = (((1,), (1,)), ((), ()))
        skip = start - first

        def gram(g, n):
            panels(g, n, lambda copy: copy.wait())
            for u in range(group):
                k = order_ref[g * group + u]
                slot = g % ring * group + u
                row = pl.ds(pl.multiple_of((k + skip) * rows, rows), rows)
                re = left[row, : n * LANES]
                im = left[row, slots : slots + n * LANES]
                lhs = jnp.concatenate([jnp.concatenate([re, im], 1), jnp.concatenate([im, -re], 1)], 0)
                rhs = jnp.concatenate([buf[slot, 0, :, : n * LANES], buf[slot, 1, :, : n * LANES]], 1)
                out = lax.dot_general(lhs, rhs, dims, preferred_element_type=jnp.float32).astype(jnp.bfloat16)
                keep_ref[k, 0] = out[:keep]
                keep_ref[k, 1] = out[rows : rows + keep]
                for j in range(splits):
                    send_refs[j][k, 0] = out[keep:rows, j * LANES : (j + 1) * LANES]
                    send_refs[j][k, 1] = out[rows + keep :, j * LANES : (j + 1) * LANES]

        def step(g, _):
            @pl.when(g + ahead < groups)
            def _():
                per_class(g + ahead, lambda n: panels(g + ahead, n, lambda copy: copy.start()))

            per_class(g, lambda n: gram(g, n))
            return 0

        lax.fori_loop(0, groups, step, 0)

    anywhere = pl.BlockSpec(memory_space=pl.ANY)
    local = pl.BlockSpec(memory_space=pltpu.VMEM)
    scalars = pl.BlockSpec(memory_space=pltpu.SMEM)
    kept = jax.ShapeDtypeStruct((count, 2, keep, columns), jnp.bfloat16)
    sent = jax.ShapeDtypeStruct((count, 2, keep, LANES), jnp.bfloat16)
    return pl.pallas_call(
        kernel,
        out_shape=(kept,) + (sent,) * splits,
        in_specs=[scalars, scalars, local] + [anywhere] * (rows + 1),
        out_specs=(local,) * (1 + splits),
        scratch_shapes=[
            pltpu.VMEM((rows, span, width), jnp.bfloat16),
            pltpu.VMEM((span * rows, 2 * slots), jnp.bfloat16),
            pltpu.VMEM((ring * group, 2, columns, slots), jnp.bfloat16),
            pltpu.SemaphoreType.DMA((rows,)),
            pltpu.SemaphoreType.DMA((ring * group,)),
        ],
        name="density_part",
    )(order, tiles, spread, *parts, orbitals)


PIECES = 4


def take_rows(which, value, keep):
    count, _, _, columns = value.shape
    size = count // PIECES

    def kernel(which_ref, value_ref, out_ref, held, in_sem, out_sem):
        rows = pl.ds(pl.multiple_of(which_ref[0] * keep, keep), keep)

        def load(i):
            part = pl.ds(i * size, size)
            return pltpu.make_async_copy(value_ref.at[part, :, rows, :], held.at[part], in_sem.at[i])

        def store(i):
            part = pl.ds(i * size, size)
            return pltpu.make_async_copy(held.at[part], out_ref.at[part], out_sem.at[i])

        for i in range(PIECES):
            load(i).start()
        for i in range(PIECES):
            load(i).wait()
            store(i).start()
        for i in range(PIECES):
            store(i).wait()

    shape = (count, 2, keep, columns)
    anywhere = pl.BlockSpec(memory_space=pl.ANY)
    return pl.pallas_call(
        kernel,
        out_shape=jax.ShapeDtypeStruct(shape, value.dtype),
        in_specs=[pl.BlockSpec(memory_space=pltpu.SMEM), anywhere],
        out_specs=anywhere,
        scratch_shapes=[
            pltpu.VMEM(shape, value.dtype),
            pltpu.SemaphoreType.DMA((PIECES,)),
            pltpu.SemaphoreType.DMA((PIECES,)),
        ],
        name="take_rows",
    )(which, value)


def add(a, b):
    return a[0] + b[0], a[1] + b[1]


def sub(a, b):
    return a[0] - b[0], a[1] - b[1]


def three(a, b, c, inverse):
    total = add(b, c)
    first = add(a, total)
    middle = a[0] - 0.5 * total[0], a[1] - 0.5 * total[1]
    turn = ROOT * (b[0] - c[0]), ROOT * (b[1] - c[1])
    low = middle[0] + turn[1], middle[1] - turn[0]
    high = middle[0] - turn[1], middle[1] + turn[0]
    return (first, high, low) if inverse else (first, low, high)


def six(x):
    u = three(add(x[0], x[3]), add(x[4], x[1]), add(x[2], x[5]), False)
    v = three(sub(x[0], x[3]), sub(x[4], x[1]), sub(x[2], x[5]), False)
    return list(u) + list(v)


def six_back(x):
    u = three(*x[:3], True)
    v = three(*x[3:], True)
    return [add(u[0], v[0]), sub(u[1], v[1]), add(u[2], v[2]), sub(u[0], v[0]), add(u[1], v[1]), sub(u[2], v[2])]


def first_pass(own, other, work):
    def load(ref, k):
        return ref[k, 0].astype(jnp.float32), ref[k, 1].astype(jnp.float32)

    for kx in range(HALF):

        def body(ky, _):
            base = ky * KSIDE + kx * KSIDE * KSIDE * (1 if len(own) == 1 else 0)
            mine = [load(own[kx % len(own)], base + kz) for kz in range(KSIDE)]
            theirs = [load(other[kx % len(other)], base + kz) for kz in range(KSIDE)]
            plus = six([add(a, b) for a, b in zip(mine, theirs)])
            minus = six([sub(b, a) if kx % 2 else sub(a, b) for a, b in zip(mine, theirs)])
            for sign, values in enumerate((plus, minus)):
                for kz in range(KSIDE):
                    for part in range(2):
                        work[sign, kz, kx, ky, part] = values[kz][part]
            return 0

        lax.fori_loop(0, KSIDE, body, 0)


def plane_forward(work, sign, kz):
    grid = []
    for kx in range(HALF):
        grid.append(six([(work[sign, kz, kx, ky, 0], work[sign, kz, kx, ky, 1]) for ky in range(KSIDE)]))
    for ky in range(KSIDE):
        column = three(grid[0][ky], grid[1][ky], grid[2][ky], False)
        for kx in range(HALF):
            grid[kx][ky] = column[kx]
    return grid


def coulomb_transform(which, coulomb, other, column):
    count, _, rows, _ = other.shape
    scale = -0.5 / (HALF * HALF * HALF * 4 * KSIDE * KSIDE * KSIDE)

    def kernel(which_ref, own_ref, other_ref, out_ref, work):
        first_pass([own_ref], [other_ref], work)
        flip = jnp.where(which_ref[0] == 0, scale, -scale).astype(jnp.float32)

        def body(kz, _):
            for sign in range(2):
                factor = flip if sign else jnp.float32(scale)
                grid = plane_forward(work, sign, kz)
                for kx in range(HALF):
                    for ky in range(KSIDE):
                        for part in range(2):
                            out_ref[sign, kz, kx, ky, part] = grid[kx][ky][part] * factor
            return 0

        lax.fori_loop(0, KSIDE, body, 0)

    shape = (2, KSIDE, HALF, KSIDE, 2, rows, LANES)
    block = (count, 2, rows, LANES)
    return pl.pallas_call(
        kernel,
        out_shape=jax.ShapeDtypeStruct(shape, jnp.float32),
        grid_spec=pltpu.PrefetchScalarGridSpec(
            num_scalar_prefetch=1,
            grid=(1,),
            in_specs=[
                pl.BlockSpec(block, lambda i, w: (0, 0, w[0], column)),
                pl.BlockSpec(block, lambda i, w: (0, 0, 0, column)),
            ],
            out_specs=pl.BlockSpec(shape, lambda i, w: (0,) * 7),
            scratch_shapes=[pltpu.VMEM(shape, jnp.float32)],
        ),
        name="coulomb_transform",
    )(which, coulomb, other)


def convolve(which, own, other, kernel_hat, column, whole):
    planes = len(own)
    rows, columns = own[0].shape[2:]
    count = sum(value.shape[0] for value in own)

    def kernel(which_ref, *refs):
        own_refs, other_refs, hat = refs[:planes], refs[planes : 2 * planes], refs[2 * planes]
        keep_ref, send_ref, work = refs[-3:]
        first_pass(own_refs, other_refs, work)

        def middle(kz, _):
            for sign in range(2):
                grid = plane_forward(work, sign, kz)
                for ky in range(KSIDE):
                    column_values = []
                    for kx in range(HALF):
                        a, b = grid[kx][ky]
                        c, d = hat[sign, kz, kx, ky, 0], hat[sign, kz, kx, ky, 1]
                        column_values.append((a * c - b * d, a * d + b * c))
                    column_values = three(*column_values, True)
                    for kx in range(HALF):
                        grid[kx][ky] = column_values[kx]
                for kx in range(HALF):
                    values = six_back(grid[kx])
                    for ky in range(KSIDE):
                        for part in range(2):
                            work[sign, kz, kx, ky, part] = values[ky][part]
            return 0

        lax.fori_loop(0, KSIDE, middle, 0)

        def last(ky, _):
            for kx in range(HALF):
                both = []
                for sign in range(2):
                    both.append(six_back([(work[sign, kz, kx, ky, 0], work[sign, kz, kx, ky, 1]) for kz in range(KSIDE)]))
                base = (kx * KSIDE + ky) * KSIDE
                for kz in range(KSIDE):
                    for part in range(2):
                        plus, minus = both[0][kz][part], both[1][kz][part]
                        if kx % 2:
                            minus = -minus
                        keep_ref[base + kz, part] = (plus + minus).astype(jnp.bfloat16)
                        send_ref[base + kz, part] = (plus - minus).astype(jnp.bfloat16)
            return 0

        lax.fori_loop(0, KSIDE, last, 0)

    shape = (2, KSIDE, HALF, KSIDE, 2, rows, LANES)
    block = (count, 2, rows, LANES)
    plane = pl.BlockSpec((count // planes, 2, rows, LANES), lambda i, w: (0, 0, 0, column))
    come = pl.BlockSpec((count // planes, 2, rows, LANES), lambda i, w: (0, 0, 0, 0))
    specs = [plane] * planes + [come] * planes + [pl.BlockSpec(shape, lambda i, w: (0,) * 7)]
    extra = () if whole is None else (whole,)
    return pl.pallas_call(
        kernel,
        out_shape=(
            jax.ShapeDtypeStruct((count, 2, 2 * rows, columns), jnp.bfloat16),
            jax.ShapeDtypeStruct(block, jnp.bfloat16),
        ),
        grid_spec=pltpu.PrefetchScalarGridSpec(
            num_scalar_prefetch=1,
            grid=(1,),
            in_specs=specs + [pl.BlockSpec(memory_space=pl.ANY)] * len(extra),
            out_specs=(
                pl.BlockSpec(block, lambda i, w: (0, 0, w[0], column)),
                pl.BlockSpec(block, lambda i, w: (0, 0, 0, 0)),
            ),
            scratch_shapes=[pltpu.VMEM(shape, jnp.float32)],
        ),
        input_output_aliases={2 + 2 * planes: 0} if extra else {},
        name="convolve",
    )(which, *own, *other, kernel_hat, *extra)


def band_gram(left, right):

    def product(first, second):
        return jnp.einsum("krb,knb->krn", first, second, preferred_element_type=jnp.float32)

    real = product(left[:, 0], right[:, 0]) + product(left[:, 1], right[:, 1])
    imag = product(left[:, 1], right[:, 0]) - product(left[:, 0], right[:, 1])
    return jnp.stack([real, imag], 1)


def side_table(sign):
    index = jnp.arange(KSIDE, dtype=jnp.int32)
    phase = index[:, None] * index[None, :] % KSIDE
    angle = phase.astype(jnp.float32) * (2.0 * jnp.pi / KSIDE)
    cosine = jnp.cos(angle)
    sine = jnp.sin(angle) * sign
    top = jnp.stack([cosine, sine], 2)
    bottom = jnp.stack([-sine, cosine], 2)
    return jnp.stack([top, bottom], 1)


def mesh_transform(values, sign):
    table = side_table(sign)
    forms = ["acbd,bxydm->axycm", "acbd,xbydm->xaycm", "acbd,xybdm->xyacm"]
    for form in forms:
        values = jnp.einsum(
            form, table, values, precision=lax.Precision.HIGHEST, preferred_element_type=jnp.float32
        )
    return values


def convolve_any(density, kernel):
    shape = density.shape
    count = shape[0]
    dens = mesh_transform(density.astype(jnp.float32).reshape(KSIDE, KSIDE, KSIDE, 2, -1), 1.0)
    kern = mesh_transform(kernel.astype(jnp.float32).reshape(KSIDE, KSIDE, KSIDE, 2, -1), 1.0)
    prod_re = kern[:, :, :, 0] * dens[:, :, :, 0] - kern[:, :, :, 1] * dens[:, :, :, 1]
    prod_im = kern[:, :, :, 0] * dens[:, :, :, 1] + kern[:, :, :, 1] * dens[:, :, :, 0]
    back = mesh_transform(jnp.stack([prod_re, prod_im], 3), -1.0)
    scale = -1.0 / (count * count)
    return (back * scale).reshape(shape).astype(jnp.bfloat16)


def slab_rows(orbitals, counts, occupation):
    slots = orbitals.shape[3]
    band = jnp.arange(slots, dtype=jnp.int32)
    weights = jnp.where(band[None, :] < counts[:, None], occupation, jnp.float32(0.0))
    return (orbitals[:, :, :ROW_DEV, :].astype(jnp.float32) * weights[:, None, None, :]).astype(
        jnp.bfloat16
    )


def local_any(orbitals, counts, occupation, coulomb):
    weighted = slab_rows(orbitals, counts, occupation)
    gathered = lax.all_gather(weighted, "pts", axis=2, tiled=True)
    density = band_gram(gathered, orbitals).astype(jnp.bfloat16)
    result = convolve_any(
        lax.all_to_all(density, "ka", split_axis=3, concat_axis=0, tiled=True),
        lax.all_to_all(coulomb, "ka", split_axis=3, concat_axis=0, tiled=True),
    )
    return lax.all_to_all(result, "ka", split_axis=0, concat_axis=3, tiled=True)


def gather_rows(block, ring):
    def move(value, dest):
        pairs = []
        for z in range(ring):
            for y in range(2):
                for core in range(2):
                    to_z, to_y, to_core = dest(z, y, core)
                    pairs.append(((z * 2 + y) * 2 + core, (to_z % ring * 2 + to_y) * 2 + to_core))
        return lax.ppermute(value, "pts", pairs)

    def twin(z, y, core):
        return z, y, 1 - core

    def along(z, y, core):
        return z + 1 - 2 * core, y, core

    def across(z, y, core):
        return z, 1 - y, core

    def corner(z, y, core):
        return z + 1 - 2 * core, 1 - y, core

    here = lax.axis_index("pts")
    core = here % 2
    y = here // 2 % 2
    z = here // 4

    def index(dz, flip_y, of_core):
        return ((z + dz) % ring * 2 + (1 - y if flip_y else y)) * 2 + of_core

    back = 2 * core - 1
    near = move(block, twin)
    side_own = move(block, along)
    corner_own = move(block, corner)
    across_own = move(block, across)
    side_twin = move(near, along)
    corner_twin = move(near, corner)
    far = move(side_own, along)
    far_corner = move(corner_own, along)
    received = [
        (side_own, back, 0, core),
        (side_twin, back, 0, 1 - core),
        (corner_own, back, 1, core),
        (corner_twin, back, 1, 1 - core),
        (across_own, 0, 1, core),
        (far, 2 * back, 0, core),
        (far_corner, 2 * back, 1, core),
    ]
    parts = [block, near]
    where = [index(0, 0, core), index(0, 0, 1 - core)]
    for value, dz, flip_y, of_core in received:
        parts.append(value)
        where.append(index(dz, flip_y, of_core))
        parts.append(move(value, twin))
        where.append(index(-dz, flip_y, 1 - of_core))
    return parts, jnp.stack(where)


def pack_block(weighted):
    count, _, _, slots = weighted.shape
    whole = slots - LANES
    re, im = weighted[:, 0, 0], weighted[:, 1, 0]
    middle = whole + LANE_HALF
    block = jnp.concatenate([re[:, :whole], im[:, :whole], re[:, whole:middle], im[:, whole:middle]], 1)
    return jnp.pad(block, ((0, -count % BLOCK), (0, 0)))


def local_pair(orbitals, counts, occupation, coulomb):
    swap = [(0, 1), (1, 0)]
    count, _, columns, _ = orbitals.shape
    rows = coulomb.shape[2]
    keep = rows // 2
    half = lax.axis_index("ka")
    mine = half.astype(jnp.int32).reshape(1)
    theirs = 1 - mine
    other_coulomb = lax.ppermute(take_rows(theirs, coulomb, keep), "ka", swap)
    block = pack_block(slab_rows(orbitals, counts, occupation))
    parts, where = gather_rows(block, lax.axis_size("pts") // 4)
    where = ((where + keep * half) % rows).astype(jnp.int32)
    place = jnp.arange(rows * BLOCK, dtype=jnp.int32)
    target = jnp.broadcast_to(where[:, None], (rows, BLOCK)).reshape(-1)
    spread = (place[:, None] // rows == place[None, :] % BLOCK) & (place[:, None] % rows == target[None, :])
    spread = spread.astype(jnp.bfloat16)
    splits = columns // LANES
    order, tiles = band_order(counts, HALF)
    order, tiles, spread = lax.optimization_barrier((order, tiles, spread))
    size = count // HALF
    own, other = [], []
    for i in range(HALF):
        kept, *sent = density_part(spread, order[i], tiles[i], parts, orbitals, i * size, size)
        own.append(kept)
        other.append([])
        for value in sent:
            other[i].append(lax.ppermute(value, "ka", swap))
    whole = None
    returned = []
    for j in range(splits):
        hat = coulomb_transform(mine, coulomb, other_coulomb, j)
        whole, sent = convolve(mine, own, [value[j] for value in other], hat, j, whole)
        returned.append(lax.ppermute(sent, "ka", swap))
    for j, value in enumerate(returned):
        whole = lax.dynamic_update_slice(whole, value, (0, 0, theirs[0] * keep, j * LANES))
    return whole


def solution(mesh):
    pair = mesh.shape["ka"] == 2 and mesh.shape["pts"] == BLOCK

    def local(orbitals, counts, occupation, coulomb):
        columns = orbitals.shape[2]
        if pair and columns % LANES == 0 and orbitals.shape[0] % (HALF * KSIDE * KSIDE) == 0:
            return local_pair(orbitals, counts, occupation, coulomb)
        return local_any(orbitals, counts, occupation, coulomb)

    return jax.shard_map(
        local,
        mesh=mesh,
        in_specs=(P("ka", None, "pts", None), P("ka"), P("ka", None), P("ka", None, None, "pts")),
        out_specs=P("ka", None, None, "pts"),
        check_vma=False,
    )
```

```python
import jax
import jax.numpy as jnp
from jax import lax
from jax.experimental import pallas as pl
from jax.experimental.pallas import tpu as pltpu
from jax.sharding import PartitionSpec as P


KSIDE = 6
ROW_DEV = 1
HALF = KSIDE // 2
LANES = 128
ROOT = 0.8660254037844386


LANE_HALF = LANES // 2
GROUP = 6
AHEAD = 2
PARTS = ((0, 2), (2, 1))
BLOCK = 16


def band_order(counts, size):
    tiles = -(-counts // LANES)
    index = jnp.arange(counts.shape[0], dtype=jnp.int32)
    part = jnp.where(index < PARTS[1][0] * size, 0, PARTS[1][0] * size)
    key = tiles * counts.shape[0] - index
    same = part[:, None] == part[None, :]
    rank = part + jnp.sum((same & (key[None, :] > key[:, None])).astype(jnp.int32), 1)
    hit = (rank[:, None] == index[None, :]).astype(jnp.int32)
    return jnp.sum(hit * (index - part)[:, None], 0), jnp.sum(hit * tiles[:, None], 0)


def density_part(spread, order, tiles, parts, orbitals, start, count, splits):
    rows = len(parts)
    width = parts[0].shape[1]
    columns, slots = orbitals.shape[2:]
    keep = rows // 2
    first = start // BLOCK * BLOCK
    span = -(-(start + count - first) // BLOCK) * BLOCK
    group = GROUP
    ahead = AHEAD
    groups = count // group
    ring = ahead + 1
    whole = (slots // LANES - 1) * LANES
    depth = slots // LANES
    chunk = columns // splits

    def kernel(order_ref, tiles_ref, spread_ref, *refs):
        sources, orb, refs = refs[:rows], refs[rows], refs[rows + 1 :]
        keep_ref, send_refs, (raw, left, buf, raw_sem, sem) = refs[0], refs[1 : 1 + splits], refs[1 + splits :]
        row_copies = [
            pltpu.make_async_copy(sources[i].at[pl.ds(first, span)], raw.at[i], raw_sem.at[i]) for i in range(rows)
        ]

        def per_class(g, act):
            for n in range(1, depth + 1):
                pl.when(tiles_ref[start + g * group] == n)(lambda n=n: act(n))

        def panels(g, n, act):
            lanes = pl.ds(0, n * LANES)
            for u in range(group):
                slot = g % ring * group + u
                source = orb.at[start + order_ref[start + g * group + u], :, :, lanes]
                act(pltpu.make_async_copy(source, buf.at[slot, :, :, lanes], sem.at[slot]))

        for copy in row_copies:
            copy.start()
        for g in range(min(ahead, groups)):
            per_class(g, lambda n, g=g: panels(g, n, lambda copy: copy.start()))
        for copy in row_copies:
            copy.wait()
        lane = lax.broadcasted_iota(jnp.int32, (BLOCK * rows, LANES), 1)
        for at in range(0, span, BLOCK):
            stacked = jnp.concatenate([raw[i, at : at + BLOCK, :] for i in range(rows)], 0)
            mixed = jnp.dot(spread_ref[...], stacked, preferred_element_type=jnp.float32)
            last = mixed[:, 2 * whole :]
            re_last = jnp.where(lane < LANE_HALF, last, 0.0)
            im_last = jnp.where(lane < LANE_HALF, pltpu.roll(last, LANE_HALF, 1), 0.0)
            pieces = [mixed[:, :whole], re_last, mixed[:, whole : 2 * whole], im_last]
            left[at * rows : (at + BLOCK) * rows, :] = jnp.concatenate(pieces, 1).astype(jnp.bfloat16)
        dims = (((1,), (1,)), ((), ()))
        skip = start - first

        def gram(g, n):
            panels(g, n, lambda copy: copy.wait())
            for u in range(group):
                k = order_ref[start + g * group + u]
                slot = g % ring * group + u
                row = pl.ds(pl.multiple_of((k + skip) * rows, rows), rows)
                re = left[row, : n * LANES]
                im = left[row, slots : slots + n * LANES]
                lhs = jnp.concatenate([jnp.concatenate([re, im], 1), jnp.concatenate([im, -re], 1)], 0)
                rhs = jnp.concatenate([buf[slot, 0, :, : n * LANES], buf[slot, 1, :, : n * LANES]], 1)
                out = lax.dot_general(lhs, rhs, dims, preferred_element_type=jnp.float32).astype(jnp.bfloat16)
                keep_ref[k, 0] = out[:keep]
                keep_ref[k, 1] = out[rows : rows + keep]
                for j in range(splits):
                    send_refs[j][k, 0] = out[keep:rows, j * chunk : (j + 1) * chunk]
                    send_refs[j][k, 1] = out[rows + keep :, j * chunk : (j + 1) * chunk]

        def step(g, _):
            @pl.when(g + ahead < groups)
            def _():
                per_class(g + ahead, lambda n: panels(g + ahead, n, lambda copy: copy.start()))

            per_class(g, lambda n: gram(g, n))
            return 0

        lax.fori_loop(0, groups, step, 0)

    anywhere = pl.BlockSpec(memory_space=pl.ANY)
    local = pl.BlockSpec(memory_space=pltpu.VMEM)
    scalars = pl.BlockSpec(memory_space=pltpu.SMEM)
    kept = jax.ShapeDtypeStruct((count, 2, keep, columns), jnp.bfloat16)
    sent = jax.ShapeDtypeStruct((count, 2, keep, chunk), jnp.bfloat16)
    return pl.pallas_call(
        kernel,
        out_shape=(kept,) + (sent,) * splits,
        in_specs=[scalars, scalars, local] + [anywhere] * (rows + 1),
        out_specs=(local,) * (1 + splits),
        scratch_shapes=[
            pltpu.VMEM((rows, span, width), jnp.bfloat16),
            pltpu.VMEM((span * rows, 2 * slots), jnp.bfloat16),
            pltpu.VMEM((ring * group, 2, columns, slots), jnp.bfloat16),
            pltpu.SemaphoreType.DMA((rows,)),
            pltpu.SemaphoreType.DMA((ring * group,)),
        ],
        name="density_part",
    )(order, tiles, spread, *parts, orbitals)


PIECES = 4


def take_rows(which, value, keep):
    count, _, _, columns = value.shape
    size = count // PIECES

    def kernel(which_ref, value_ref, out_ref, held, in_sem, out_sem):
        rows = pl.ds(pl.multiple_of(which_ref[0] * keep, keep), keep)

        def load(i):
            part = pl.ds(i * size, size)
            return pltpu.make_async_copy(value_ref.at[part, :, rows, :], held.at[part], in_sem.at[i])

        def store(i):
            part = pl.ds(i * size, size)
            return pltpu.make_async_copy(held.at[part], out_ref.at[part], out_sem.at[i])

        for i in range(PIECES):
            load(i).start()
        for i in range(PIECES):
            load(i).wait()
            store(i).start()
        for i in range(PIECES):
            store(i).wait()

    shape = (count, 2, keep, columns)
    anywhere = pl.BlockSpec(memory_space=pl.ANY)
    return pl.pallas_call(
        kernel,
        out_shape=jax.ShapeDtypeStruct(shape, value.dtype),
        in_specs=[pl.BlockSpec(memory_space=pltpu.SMEM), anywhere],
        out_specs=anywhere,
        scratch_shapes=[
            pltpu.VMEM(shape, value.dtype),
            pltpu.SemaphoreType.DMA((PIECES,)),
            pltpu.SemaphoreType.DMA((PIECES,)),
        ],
        name="take_rows",
    )(which, value)


def add(a, b):
    return a[0] + b[0], a[1] + b[1]


def sub(a, b):
    return a[0] - b[0], a[1] - b[1]


def three(a, b, c, inverse):
    total = add(b, c)
    first = add(a, total)
    middle = a[0] - 0.5 * total[0], a[1] - 0.5 * total[1]
    turn = ROOT * (b[0] - c[0]), ROOT * (b[1] - c[1])
    low = middle[0] + turn[1], middle[1] - turn[0]
    high = middle[0] - turn[1], middle[1] + turn[0]
    return (first, high, low) if inverse else (first, low, high)


def six(x):
    u = three(add(x[0], x[3]), add(x[4], x[1]), add(x[2], x[5]), False)
    v = three(sub(x[0], x[3]), sub(x[4], x[1]), sub(x[2], x[5]), False)
    return list(u) + list(v)


def six_back(x):
    u = three(*x[:3], True)
    v = three(*x[3:], True)
    return [add(u[0], v[0]), sub(u[1], v[1]), add(u[2], v[2]), sub(u[0], v[0]), add(u[1], v[1]), sub(u[2], v[2])]


def first_pass(own, other, work):
    def load(ref, k):
        return ref[k, 0].astype(jnp.float32), ref[k, 1].astype(jnp.float32)

    for kx in range(HALF):

        def body(ky, _):
            part = max(i for i in range(len(own)) if PARTS[i][0] <= kx)
            base = ky * KSIDE + (kx - PARTS[part][0]) * KSIDE * KSIDE
            mine = [load(own[part], base + kz) for kz in range(KSIDE)]
            theirs = [load(other[part], base + kz) for kz in range(KSIDE)]
            plus = six([add(a, b) for a, b in zip(mine, theirs)])
            minus = six([sub(b, a) if kx % 2 else sub(a, b) for a, b in zip(mine, theirs)])
            for sign, values in enumerate((plus, minus)):
                for kz in range(KSIDE):
                    for part in range(2):
                        work[sign, kz, kx, ky, part] = values[kz][part]
            return 0

        lax.fori_loop(0, KSIDE, body, 0)


def plane_forward(work, sign, kz):
    grid = []
    for kx in range(HALF):
        grid.append(six([(work[sign, kz, kx, ky, 0], work[sign, kz, kx, ky, 1]) for ky in range(KSIDE)]))
    for ky in range(KSIDE):
        column = three(grid[0][ky], grid[1][ky], grid[2][ky], False)
        for kx in range(HALF):
            grid[kx][ky] = column[kx]
    return grid


def coulomb_transform(which, coulomb, other, column):
    count, _, rows, _ = other.shape
    scale = -0.5 / (HALF * HALF * HALF * 4 * KSIDE * KSIDE * KSIDE)

    def kernel(which_ref, own_ref, other_ref, out_ref, work):
        first_pass([own_ref], [other_ref], work)
        flip = jnp.where(which_ref[0] == 0, scale, -scale).astype(jnp.float32)

        def body(kz, _):
            for sign in range(2):
                factor = flip if sign else jnp.float32(scale)
                grid = plane_forward(work, sign, kz)
                for kx in range(HALF):
                    for ky in range(KSIDE):
                        for part in range(2):
                            out_ref[sign, kz, kx, ky, part] = grid[kx][ky][part] * factor
            return 0

        lax.fori_loop(0, KSIDE, body, 0)

    shape = (2, KSIDE, HALF, KSIDE, 2, rows, LANES)
    block = (count, 2, rows, LANES)
    return pl.pallas_call(
        kernel,
        out_shape=jax.ShapeDtypeStruct(shape, jnp.float32),
        grid_spec=pltpu.PrefetchScalarGridSpec(
            num_scalar_prefetch=1,
            grid=(1,),
            in_specs=[
                pl.BlockSpec(block, lambda i, w: (0, 0, w[0], column)),
                pl.BlockSpec(block, lambda i, w: (0, 0, 0, column)),
            ],
            out_specs=pl.BlockSpec(shape, lambda i, w: (0,) * 7),
            scratch_shapes=[pltpu.VMEM(shape, jnp.float32)],
        ),
        name="coulomb_transform",
    )(which, coulomb, other)


def convolve(which, own, other, kernel_hat, column, whole):
    planes = len(own)
    rows, columns = own[0].shape[2:]
    count = sum(value.shape[0] for value in own)

    def kernel(which_ref, *refs):
        own_refs, other_refs, hat = refs[:planes], refs[planes : 2 * planes], refs[2 * planes]
        keep_ref, send_ref, work = refs[-3:]
        first_pass(own_refs, other_refs, work)

        def middle(kz, _):
            for sign in range(2):
                grid = plane_forward(work, sign, kz)
                for ky in range(KSIDE):
                    column_values = []
                    for kx in range(HALF):
                        a, b = grid[kx][ky]
                        c, d = hat[sign, kz, kx, ky, 0], hat[sign, kz, kx, ky, 1]
                        column_values.append((a * c - b * d, a * d + b * c))
                    column_values = three(*column_values, True)
                    for kx in range(HALF):
                        grid[kx][ky] = column_values[kx]
                for kx in range(HALF):
                    values = six_back(grid[kx])
                    for ky in range(KSIDE):
                        for part in range(2):
                            work[sign, kz, kx, ky, part] = values[ky][part]
            return 0

        lax.fori_loop(0, KSIDE, middle, 0)

        def last(ky, _):
            for kx in range(HALF):
                both = []
                for sign in range(2):
                    both.append(six_back([(work[sign, kz, kx, ky, 0], work[sign, kz, kx, ky, 1]) for kz in range(KSIDE)]))
                base = (kx * KSIDE + ky) * KSIDE
                for kz in range(KSIDE):
                    for part in range(2):
                        plus, minus = both[0][kz][part], both[1][kz][part]
                        if kx % 2:
                            minus = -minus
                        keep_ref[base + kz, part] = (plus + minus).astype(jnp.bfloat16)
                        send_ref[base + kz, part] = (plus - minus).astype(jnp.bfloat16)
            return 0

        lax.fori_loop(0, KSIDE, last, 0)

    shape = (2, KSIDE, HALF, KSIDE, 2, rows, LANES)
    block = (count, 2, rows, LANES)

    def plane(value):
        at = column if value.shape[3] == columns else 0
        return pl.BlockSpec(value.shape[:3] + (LANES,), lambda i, w: (0, 0, 0, at))

    specs = [plane(value) for value in (*own, *other)] + [pl.BlockSpec(shape, lambda i, w: (0,) * 7)]
    extra = () if whole is None else (whole,)
    return pl.pallas_call(
        kernel,
        out_shape=(
            jax.ShapeDtypeStruct((count, 2, 2 * rows, columns), jnp.bfloat16),
            jax.ShapeDtypeStruct(block, jnp.bfloat16),
        ),
        grid_spec=pltpu.PrefetchScalarGridSpec(
            num_scalar_prefetch=1,
            grid=(1,),
            in_specs=specs + [pl.BlockSpec(memory_space=pl.ANY)] * len(extra),
            out_specs=(
                pl.BlockSpec(block, lambda i, w: (0, 0, w[0], column)),
                pl.BlockSpec(block, lambda i, w: (0, 0, 0, 0)),
            ),
            scratch_shapes=[pltpu.VMEM(shape, jnp.float32)],
        ),
        input_output_aliases={2 + 2 * planes: 0} if extra else {},
        name="convolve",
    )(which, *own, *other, kernel_hat, *extra)


def band_gram(left, right):

    def product(first, second):
        return jnp.einsum("krb,knb->krn", first, second, preferred_element_type=jnp.float32)

    real = product(left[:, 0], right[:, 0]) + product(left[:, 1], right[:, 1])
    imag = product(left[:, 1], right[:, 0]) - product(left[:, 0], right[:, 1])
    return jnp.stack([real, imag], 1)


def side_table(sign):
    index = jnp.arange(KSIDE, dtype=jnp.int32)
    phase = index[:, None] * index[None, :] % KSIDE
    angle = phase.astype(jnp.float32) * (2.0 * jnp.pi / KSIDE)
    cosine = jnp.cos(angle)
    sine = jnp.sin(angle) * sign
    top = jnp.stack([cosine, sine], 2)
    bottom = jnp.stack([-sine, cosine], 2)
    return jnp.stack([top, bottom], 1)


def mesh_transform(values, sign):
    table = side_table(sign)
    forms = ["acbd,bxydm->axycm", "acbd,xbydm->xaycm", "acbd,xybdm->xyacm"]
    for form in forms:
        values = jnp.einsum(
            form, table, values, precision=lax.Precision.HIGHEST, preferred_element_type=jnp.float32
        )
    return values


def convolve_any(density, kernel):
    shape = density.shape
    count = shape[0]
    dens = mesh_transform(density.astype(jnp.float32).reshape(KSIDE, KSIDE, KSIDE, 2, -1), 1.0)
    kern = mesh_transform(kernel.astype(jnp.float32).reshape(KSIDE, KSIDE, KSIDE, 2, -1), 1.0)
    prod_re = kern[:, :, :, 0] * dens[:, :, :, 0] - kern[:, :, :, 1] * dens[:, :, :, 1]
    prod_im = kern[:, :, :, 0] * dens[:, :, :, 1] + kern[:, :, :, 1] * dens[:, :, :, 0]
    back = mesh_transform(jnp.stack([prod_re, prod_im], 3), -1.0)
    scale = -1.0 / (count * count)
    return (back * scale).reshape(shape).astype(jnp.bfloat16)


def slab_rows(orbitals, counts, occupation):
    slots = orbitals.shape[3]
    band = jnp.arange(slots, dtype=jnp.int32)
    weights = jnp.where(band[None, :] < counts[:, None], occupation, jnp.float32(0.0))
    return (orbitals[:, :, :ROW_DEV, :].astype(jnp.float32) * weights[:, None, None, :]).astype(
        jnp.bfloat16
    )


def local_any(orbitals, counts, occupation, coulomb):
    weighted = slab_rows(orbitals, counts, occupation)
    gathered = lax.all_gather(weighted, "pts", axis=2, tiled=True)
    density = band_gram(gathered, orbitals).astype(jnp.bfloat16)
    result = convolve_any(
        lax.all_to_all(density, "ka", split_axis=3, concat_axis=0, tiled=True),
        lax.all_to_all(coulomb, "ka", split_axis=3, concat_axis=0, tiled=True),
    )
    return lax.all_to_all(result, "ka", split_axis=0, concat_axis=3, tiled=True)


def gather_rows(block, ring):
    def move(value, dest):
        pairs = []
        for z in range(ring):
            for y in range(2):
                for core in range(2):
                    to_z, to_y, to_core = dest(z, y, core)
                    pairs.append(((z * 2 + y) * 2 + core, (to_z % ring * 2 + to_y) * 2 + to_core))
        return lax.ppermute(value, "pts", pairs)

    def twin(z, y, core):
        return z, y, 1 - core

    def along(z, y, core):
        return z + 1 - 2 * core, y, core

    def across(z, y, core):
        return z, 1 - y, core

    def corner(z, y, core):
        return z + 1 - 2 * core, 1 - y, core

    here = lax.axis_index("pts")
    core = here % 2
    y = here // 2 % 2
    z = here // 4

    def index(dz, flip_y, of_core):
        return ((z + dz) % ring * 2 + (1 - y if flip_y else y)) * 2 + of_core

    back = 2 * core - 1
    near = move(block, twin)
    side_own = move(block, along)
    corner_own = move(block, corner)
    across_own = move(block, across)
    side_twin = move(near, along)
    corner_twin = move(near, corner)
    far = move(side_own, along)
    far_corner = move(corner_own, along)
    received = [
        (side_own, back, 0, core),
        (side_twin, back, 0, 1 - core),
        (corner_own, back, 1, core),
        (corner_twin, back, 1, 1 - core),
        (across_own, 0, 1, core),
        (far, 2 * back, 0, core),
        (far_corner, 2 * back, 1, core),
    ]
    parts = [block, near]
    where = [index(0, 0, core), index(0, 0, 1 - core)]
    for value, dz, flip_y, of_core in received:
        parts.append(value)
        where.append(index(dz, flip_y, of_core))
        parts.append(move(value, twin))
        where.append(index(-dz, flip_y, 1 - of_core))
    return parts, jnp.stack(where)


def pack_block(weighted):
    count, _, _, slots = weighted.shape
    whole = slots - LANES
    re, im = weighted[:, 0, 0], weighted[:, 1, 0]
    middle = whole + LANE_HALF
    block = jnp.concatenate([re[:, :whole], im[:, :whole], re[:, whole:middle], im[:, whole:middle]], 1)
    return jnp.pad(block, ((0, -count % BLOCK), (0, 0)))


def local_pair(orbitals, counts, occupation, coulomb):
    swap = [(0, 1), (1, 0)]
    _, _, columns, _ = orbitals.shape
    rows = coulomb.shape[2]
    keep = rows // 2
    half = lax.axis_index("ka")
    mine = half.astype(jnp.int32).reshape(1)
    theirs = 1 - mine
    other_coulomb = lax.ppermute(take_rows(theirs, coulomb, keep), "ka", swap)
    block = pack_block(slab_rows(orbitals, counts, occupation))
    parts, where = gather_rows(block, lax.axis_size("pts") // 4)
    where = ((where + keep * half) % rows).astype(jnp.int32)
    place = jnp.arange(rows * BLOCK, dtype=jnp.int32)
    target = jnp.broadcast_to(where[:, None], (rows, BLOCK)).reshape(-1)
    spread = (place[:, None] // rows == place[None, :] % BLOCK) & (place[:, None] % rows == target[None, :])
    spread = spread.astype(jnp.bfloat16)
    splits = columns // LANES
    size = KSIDE * KSIDE
    order, tiles = band_order(counts, size)
    order, tiles, spread = lax.optimization_barrier((order, tiles, spread))
    own, other = [], []
    for i, (plane, planes) in enumerate(PARTS):
        cuts = 1 if i + 1 < len(PARTS) else splits
        kept, *sent = density_part(spread, order, tiles, parts, orbitals, plane * size, planes * size, cuts)
        own.append(kept)
        other.append([])
        for value in sent:
            other[i].append(lax.ppermute(value, "ka", swap))
    other[:-1] = [value * splits for value in other[:-1]]
    whole = None
    returned = []
    for j in range(splits):
        hat = coulomb_transform(mine, coulomb, other_coulomb, j)
        whole, sent = convolve(mine, own, [value[j] for value in other], hat, j, whole)
        returned.append(lax.ppermute(sent, "ka", swap))
    for j, value in enumerate(returned):
        whole = lax.dynamic_update_slice(whole, value, (0, 0, theirs[0] * keep, j * LANES))
    return whole


def solution(mesh):
    pair = mesh.shape["ka"] == 2 and mesh.shape["pts"] == BLOCK

    def local(orbitals, counts, occupation, coulomb):
        columns = orbitals.shape[2]
        if pair and columns % LANES == 0 and orbitals.shape[0] % (HALF * KSIDE * KSIDE) == 0:
            return local_pair(orbitals, counts, occupation, coulomb)
        return local_any(orbitals, counts, occupation, coulomb)

    return jax.shard_map(
        local,
        mesh=mesh,
        in_specs=(P("ka", None, "pts", None), P("ka"), P("ka", None), P("ka", None, None, "pts")),
        out_specs=P("ka", None, None, "pts"),
        check_vma=False,
    )
```
